32 devices in a mesh: ccd: 4 (over z), tile: 8 (over y, x, core).
Axes of the slice: x: 2, y: 2, z: 4, core: 2. Of those that a mesh axis runs over, the one named last changes fastest.
Arguments:
- frames: bfloat16 [256, 512, 128], P(None, ('ccd', 'tile')), may hold values from -24 to 24
- source_mask: int32 [256, 512, 128], P(None, ('ccd', 'tile')), may hold values 0 or 1
- good_pixels: int32 [512, 128], P(('ccd', 'tile')), may hold values 0 or 1
Outputs:
- factor: float32 [256, 256], replicated
- basis: bfloat16 [256, 512, 128], P(None, ('ccd', 'tile'))
The draws below stay inside these ranges and needn't reach their ends.
All inputs are finite; a program needn't handle non-finite values. No bound on the sum of `source_mask` or of `good_pixels` on one device may be relied on, other than what follows from the above.
Results may differ from the reference program's by a relative error of at most 0.00065.
Values may be sent and summed in bfloat16 or wider, within the bound.
A program may use at most 64 MiB of HBM per device.

```python
import math
import jax
import jax.numpy as jnp
from jax import lax

EXPOSURES = 256
REACH = 16
TILE_COLS = 128
CCDS = 2
ROWS = 256
ALL_ROWS = 512
PIXELS = 65536


def draw_frames(key, part):
    keys = jax.random.split(jax.random.fold_in(key, 11), 3)
    shape = (EXPOSURES, ALL_ROWS, TILE_COLS)
    base = jax.random.normal(keys[0], shape, jnp.float32)
    exposure_scale = 0.3 * jnp.exp(jax.random.uniform(keys[1], (EXPOSURES, 1, 1), jnp.float32, 0.0, math.log(10.0)))
    pixel_scale = jnp.exp(jax.random.uniform(keys[2], (1, ALL_ROWS, TILE_COLS), jnp.float32, math.log(0.3), math.log(3.0)))
    values = base * exposure_scale * pixel_scale
    return jnp.clip(values, -24.0, 24.0).astype(jnp.bfloat16)


def plant(drawn, stream_key, low, largest):
    extent = drawn.shape
    spot = [jax.random.randint(jax.random.fold_in(stream_key, axis), (), 0, extent[axis]) for axis in range(len(extent))]
    drawn = drawn.at[tuple(spot)].set(low)
    longest = extent.index(max(extent))
    spot[longest] = (spot[longest] + 1) % extent[longest]
    return drawn.at[tuple(spot)].set(largest)


def setup_inputs(seed: int = 0) -> dict:
    key_list = jax.random.split(jax.random.key(seed), 4)
    frames = draw_frames(jax.random.fold_in(key_list[3], 71), 0)
    source_mask = plant((jax.random.randint(key_list[1], (EXPOSURES, ALL_ROWS, TILE_COLS), 0, 8) < 7).astype(jnp.int32), jax.random.fold_in(key_list[1], 1), 0, 1)
    good_pixels = plant((jax.random.randint(key_list[2], (ALL_ROWS, TILE_COLS), 0, 16) < 15).astype(jnp.int32), jax.random.fold_in(key_list[2], 1), 0, 1)
    return dict(frames=frames, source_mask=source_mask, good_pixels=good_pixels)


def kernel_taps():
    offsets = jnp.arange(-REACH, REACH + 1).astype(jnp.float32)
    raw = jnp.exp(-jnp.abs(offsets) / 6.0)
    return raw / jnp.sqrt(jnp.sum(raw * raw))

def smooth_ccd(frames, source_mask, good_pixels, index):
    start = (index * ROWS).astype(jnp.int32)
    row_ids = start - REACH + jnp.arange(ROWS + 2 * REACH).astype(jnp.int32)
    valid = jnp.logical_and(row_ids >= 0, row_ids < ALL_ROWS)
    clipped = jnp.clip(row_ids, 0, ALL_ROWS - 1).astype(jnp.int32)
    valid_f = valid.astype(jnp.float32)
    frame_block = jnp.take(frames, clipped, axis=1).astype(jnp.float32)
    source_block = jnp.take(source_mask, clipped, axis=1).astype(jnp.float32)
    good_block = jnp.take(good_pixels, clipped, axis=0).astype(jnp.float32)[None]
    padded = frame_block * source_block * good_block * valid_f.reshape(1, ROWS + 2 * REACH, 1)
    taps = kernel_taps()
    rows_done = jnp.zeros((EXPOSURES, ROWS, TILE_COLS), jnp.float32)
    for offset in range(2 * REACH + 1):
        rows_done = rows_done + taps[offset] * padded[:, offset:offset + ROWS, :]
    padded = jnp.pad(rows_done, ((0, 0), (0, 0), (REACH, REACH)))
    smoothed = jnp.zeros((EXPOSURES, ROWS, TILE_COLS), jnp.float32)
    for offset in range(2 * REACH + 1):
        smoothed = smoothed + taps[offset] * padded[:, :, offset:offset + TILE_COLS]
    return smoothed.reshape(EXPOSURES, ROWS * TILE_COLS)

def reference(frames, source_mask, good_pixels):

    def add_gram(total, index):
        flat = smooth_ccd(frames, source_mask, good_pixels, index)
        part_gram = jnp.einsum('ep,fp->ef', flat, flat, precision=lax.Precision.HIGHEST)
        return (total + part_gram, None)
    indices = jnp.arange(CCDS).astype(jnp.int32)
    gram_sum, _ = lax.scan(add_gram, jnp.zeros((EXPOSURES, EXPOSURES), jnp.float32), indices)
    gram = gram_sum / PIXELS
    lower = jnp.linalg.cholesky(gram)
    factor = lower.T

    def solve_ccd(index):
        flat = smooth_ccd(frames, source_mask, good_pixels, index)
        solved = lax.linalg.triangular_solve(lower, flat, left_side=True, lower=True)
        return solved.astype(jnp.bfloat16).reshape(EXPOSURES, ROWS, TILE_COLS)
    stacked = lax.map(solve_ccd, indices)
    basis = jnp.moveaxis(stacked, 0, 1).reshape(EXPOSURES, ALL_ROWS, TILE_COLS)
    return (factor, basis)
```

```python
import functools

import jax
import jax.numpy as jnp
from jax import lax
from jax.experimental import pallas as pl
from jax.experimental.pallas import tpu as pltpu
from jax.sharding import PartitionSpec as P

REACH = 16
MESH = pl.DeviceIdType.MESH
HIGH = lax.Precision.HIGHEST
LANES = 128


def padded_2(array, sides, width):
    for axis, dim in sides:
        peers, length = (lax.axis_size(axis), array.shape[dim])
        up = [(i, (i + 1) % peers) for i in range(peers - 1)]
        down = [(j, i) for i, j in up]
        last = lax.slice_in_dim(array, length - width, length, axis=dim)
        first = lax.slice_in_dim(array, 0, width, axis=dim)
        before = lax.ppermute(last, axis, up)
        after = lax.ppermute(first, axis, down)
        array = jnp.concatenate([before, array, after], axis=dim)
    return array


def tap_weight(distance):
    offsets = jnp.arange(-REACH, REACH + 1).astype(jnp.float32)
    norm_sum = jnp.sqrt(jnp.sum(jnp.exp(-2.0 * jnp.abs(offsets) / 6.0)))
    inside = jnp.abs(distance) <= REACH
    return jnp.where(inside, jnp.exp(-jnp.abs(distance).astype(jnp.float32) / 6.0) / norm_sum, 0.0)


def row_matrix(tile_rows):
    out_rows = jnp.arange(tile_rows).reshape(tile_rows, 1)
    in_rows = jnp.arange(tile_rows + 2 * REACH).reshape(1, tile_rows + 2 * REACH)
    return tap_weight(in_rows - out_rows - REACH)


def column_matrix(tile_cols):
    in_cols = jnp.arange(tile_cols).reshape(tile_cols, 1)
    out_cols = jnp.arange(tile_cols).reshape(1, tile_cols)
    return tap_weight(in_cols - out_cols)


def along_rows(padded, weights):
    return jnp.einsum(
        "ip,epw->eiw", weights, padded, precision=HIGH, preferred_element_type=jnp.float32
    )


def along_columns(block, weights):
    return jnp.einsum(
        "eiv,vw->eiw", block, weights, precision=HIGH, preferred_element_type=jnp.float32
    )


def local_gram(flat):
    return jnp.einsum("ep,fp->ef", flat, flat, precision=HIGH, preferred_element_type=jnp.float32)


def sum_kernel(ccds, tiles, p_ref, o_ref, near, far, whole, s1, r1, s2, r2, s3, r3):
    c, t = lax.axis_index("ccd"), lax.axis_index("tile")
    barrier = pltpu.get_barrier_semaphore()
    for d in range(1, tiles):
        pl.semaphore_signal(barrier, inc=1, device_id=(c, lax.rem(t + d, tiles)), device_id_type=MESH)
    for d in range(1, ccds):
        pl.semaphore_signal(barrier, inc=1, device_id=(lax.rem(c + d, ccds), t), device_id_type=MESH)
    pl.semaphore_wait(barrier, tiles + ccds - 2)
    first = []
    for d in range(1, tiles):
        peer = lax.rem(t + d, tiles)
        copy = pltpu.make_async_remote_copy(
            src_ref=p_ref.at[peer], dst_ref=near.at[d - 1], send_sem=s1.at[d - 1], recv_sem=r1.at[d - 1],
            device_id=(c, peer), device_id_type=MESH)
        copy.start()
        first.append(copy)
    total = p_ref[t]
    for d in range(1, tiles):
        first[d - 1].wait_recv()
        total = total + near[d - 1]
    far[c] = total
    second = []
    for d in range(1, ccds):
        copy = pltpu.make_async_remote_copy(
            src_ref=far.at[c], dst_ref=far.at[c], send_sem=s2.at[d - 1], recv_sem=r2.at[d - 1],
            device_id=(lax.rem(c + d, ccds), t), device_id_type=MESH)
        copy.start()
        second.append(copy)
    for copy in second:
        copy.wait_recv()
    total = far[0]
    for i in range(1, ccds):
        total = total + far[i]
    whole[t] = total
    third = []
    for d in range(1, tiles):
        copy = pltpu.make_async_remote_copy(
            src_ref=whole.at[t], dst_ref=whole.at[t], send_sem=s3.at[d - 1], recv_sem=r3.at[d - 1],
            device_id=(c, lax.rem(t + d, tiles)), device_id_type=MESH)
        copy.start()
        third.append(copy)
    for copy in third:
        copy.wait_recv()
    o_ref[...] = whole[...]
    for copy in first + second + third:
        copy.wait_send()


def total_over_devices(parts):
    ccds, tiles = lax.axis_size("ccd"), lax.axis_size("tile")
    rows = parts.shape[1]
    dma = pltpu.SemaphoreType.DMA
    return pl.pallas_call(
        functools.partial(sum_kernel, ccds, tiles),
        out_shape=jax.ShapeDtypeStruct(parts.shape, jnp.float32),
        in_specs=[pl.BlockSpec(memory_space=pltpu.VMEM)],
        out_specs=pl.BlockSpec(memory_space=pltpu.VMEM),
        scratch_shapes=[
            pltpu.VMEM((tiles - 1, rows, LANES), jnp.float32),
            pltpu.VMEM((ccds, rows, LANES), jnp.float32),
            pltpu.VMEM((tiles, rows, LANES), jnp.float32),
            dma((tiles - 1,)), dma((tiles - 1,)),
            dma((ccds - 1,)), dma((ccds - 1,)),
            dma((tiles - 1,)), dma((tiles - 1,)),
        ],
        compiler_params=pltpu.CompilerParams(collective_id=0, has_side_effects=True),
    )(parts)


def matmul(a, b, contract=(1, 0)):
    return lax.dot_general(
        a, b, (((contract[0],), (contract[1],)), ((), ())), precision=HIGH, preferred_element_type=jnp.float32
    )


def factor_block(block, rows_ref):
    groups = LANES // 8
    live = [block[8 * g:8 * g + 8, :] for g in range(groups)]
    lane = lax.broadcasted_iota(jnp.int32, (8, LANES), 1)
    sub = lax.broadcasted_iota(jnp.int32, (8, LANES), 0)
    for j in range(LANES):
        g, s = divmod(j, 8)
        row = jnp.broadcast_to(live[g][s:s + 1, :], (8, LANES))
        pivot = jnp.broadcast_to(row[:, j:j + 1], (8, LANES))
        at = lane == j
        inv = 1.0 / pivot
        scaled = jnp.where(at, inv, row * inv)
        for i in range(g, groups):
            if i == g and s == 7:
                continue
            mult = jnp.broadcast_to(live[i][:, j:j + 1], (8, LANES))
            new = jnp.where(at, 0.0, live[i]) - mult * scaled
            live[i] = jnp.where(sub > s, new, live[i]) if i == g else new
        root = lax.rsqrt(pivot)
        root = root * (1.5 - 0.5 * pivot * root * root)
        rows_ref[j:j + 1, :] = (row * root)[:1, :]
    done = rows_ref[...]
    row_id = lax.broadcasted_iota(jnp.int32, (LANES, LANES), 0)
    col_id = lax.broadcasted_iota(jnp.int32, (LANES, LANES), 1)
    upper = jnp.where(col_id >= row_id, done, 0.0)
    inverse = jnp.where(col_id < row_id, done, jnp.where(col_id == row_id, 1.0 / done, 0.0))
    return upper, inverse


def solve_kernel(g_ref, a_ref, f_ref, b_ref, rows_ref, x_ref, out32):
    h = LANES
    upper, inv1 = factor_block(g_ref[0], rows_ref)
    f_ref[:h, :h] = upper
    f_ref[h:, :h] = jnp.zeros((h, h), jnp.float32)
    low = matmul(g_ref[1], inv1, (1, 1))
    f_ref[:h, h:] = low.T
    rest = g_ref[2] - matmul(low, low, (1, 1))
    upper, inv2 = factor_block(rest, rows_ref)
    f_ref[h:, h:] = upper
    x_ref[:h, :h] = inv1
    x_ref[:h, h:] = jnp.zeros((h, h), jnp.float32)
    x_ref[h:, h:] = inv2
    x_ref[h:, :h] = -matmul(inv2, matmul(low, inv1))
    exposures, pixels = a_ref.shape
    tile_rows = pixels // LANES
    for k in range(tile_rows // 2):
        part = matmul(x_ref[...], a_ref[:, 2 * k * LANES:2 * (k + 1) * LANES])
        for i in range(2):
            out32[pl.ds(2 * k + i, exposures, stride=tile_rows), :] = part[:, i * LANES:(i + 1) * LANES]
    b_ref[...] = out32[...].astype(jnp.bfloat16)


def solve(gram, flat):
    exposures, pixels = flat.shape
    vm = pl.BlockSpec(memory_space=pltpu.VMEM)
    return pl.pallas_call(
        solve_kernel,
        out_shape=(
            jax.ShapeDtypeStruct((exposures, exposures), jnp.float32),
            jax.ShapeDtypeStruct((exposures * pixels // LANES, LANES), jnp.bfloat16),
        ),
        in_specs=[vm, vm],
        out_specs=(vm, vm),
        scratch_shapes=[
            pltpu.VMEM((LANES, LANES), jnp.float32),
            pltpu.VMEM((exposures, exposures), jnp.float32),
            pltpu.VMEM((exposures * pixels // LANES, LANES), jnp.float32),
        ],
    )(gram, flat)


def per_device(frames, source_mask, good_pixels):
    exposures, tile_rows, tile_cols = frames.shape
    masked = frames * source_mask.astype(jnp.bfloat16) * good_pixels.astype(jnp.bfloat16)[None]
    rows_weights = row_matrix(tile_rows)
    cols_weights = column_matrix(tile_cols)
    padded = padded_2(masked, ((("ccd", "tile"), 1),), REACH)
    smoothed = along_columns(along_rows(padded.astype(jnp.float32), rows_weights), cols_weights)
    flat = smoothed.reshape(exposures, tile_rows * tile_cols)
    tiles = lax.axis_size("tile")
    pixel_total = float(tile_rows * tile_cols * lax.axis_size("ccd") * tiles)
    part = local_gram(flat)
    packed = jnp.stack([part[:LANES, :LANES], part[LANES:, :LANES], part[LANES:, LANES:]])
    summed = total_over_devices(packed.reshape(tiles, 3 * LANES // tiles, LANES))
    gram = summed.reshape(3, LANES, LANES) / pixel_total
    factor, basis = solve(gram, flat)
    return (factor, basis.reshape(exposures, tile_rows, tile_cols))


def solution(mesh):
    in_specs = (
        P(None, ("ccd", "tile"), None),
        P(None, ("ccd", "tile"), None),
        P(("ccd", "tile"), None),
    )
    out_specs = (P(), P(None, ("ccd", "tile"), None))
    return jax.shard_map(
        per_device, mesh=mesh, in_specs=in_specs, out_specs=out_specs, check_vma=False
    )
```

```python
import functools
import math

import jax
import jax.numpy as jnp
from jax import lax
from jax.experimental import pallas as pl
from jax.experimental.pallas import tpu as pltpu
from jax.sharding import PartitionSpec as P

REACH = 16
MESH = pl.DeviceIdType.MESH
HIGH = lax.Precision.HIGHEST
LANES = 128


def tap_weight(distance):
    offsets = jnp.arange(-REACH, REACH + 1).astype(jnp.float32)
    norm_sum = jnp.sqrt(jnp.sum(jnp.exp(-2.0 * jnp.abs(offsets) / 6.0)))
    inside = jnp.abs(distance) <= REACH
    return jnp.where(inside, jnp.exp(-jnp.abs(distance).astype(jnp.float32) / 6.0) / norm_sum, 0.0)


def column_matrix(tile_cols):
    in_cols = jnp.arange(tile_cols).reshape(tile_cols, 1)
    out_cols = jnp.arange(tile_cols).reshape(1, tile_cols)
    weights = tap_weight(in_cols - out_cols)
    offsets = jnp.arange(-REACH, REACH + 1).astype(jnp.float32)
    return weights / jnp.sqrt(jnp.sum(jnp.exp(-2.0 * jnp.abs(offsets) / 6.0)))


def sum_kernel(ccds, tiles, p_ref, o_ref, near, far, whole, s1, r1, s2, r2, s3, r3):
    c, t = lax.axis_index("ccd"), lax.axis_index("tile")
    barrier = pltpu.get_barrier_semaphore()
    for d in range(1, tiles):
        pl.semaphore_signal(barrier, inc=1, device_id=(c, lax.rem(t + d, tiles)), device_id_type=MESH)
    for d in range(1, ccds):
        pl.semaphore_signal(barrier, inc=1, device_id=(lax.rem(c + d, ccds), t), device_id_type=MESH)
    pl.semaphore_wait(barrier, tiles + ccds - 2)
    first = []
    for d in range(1, tiles):
        peer = lax.rem(t + d, tiles)
        copy = pltpu.make_async_remote_copy(
            src_ref=p_ref.at[peer], dst_ref=near.at[d - 1], send_sem=s1.at[d - 1], recv_sem=r1.at[d - 1],
            device_id=(c, peer), device_id_type=MESH)
        copy.start()
        first.append(copy)
    total = p_ref[t]
    for d in range(1, tiles):
        first[d - 1].wait_recv()
        total = total + near[d - 1]
    far[c] = total
    second = []
    for d in range(1, ccds):
        copy = pltpu.make_async_remote_copy(
            src_ref=far.at[c], dst_ref=far.at[c], send_sem=s2.at[d - 1], recv_sem=r2.at[d - 1],
            device_id=(lax.rem(c + d, ccds), t), device_id_type=MESH)
        copy.start()
        second.append(copy)
    for copy in second:
        copy.wait_recv()
    total = far[0]
    for i in range(1, ccds):
        total = total + far[i]
    whole[t] = total
    third = []
    for d in range(1, tiles):
        copy = pltpu.make_async_remote_copy(
            src_ref=whole.at[t], dst_ref=whole.at[t], send_sem=s3.at[d - 1], recv_sem=r3.at[d - 1],
            device_id=(c, lax.rem(t + d, tiles)), device_id_type=MESH)
        copy.start()
        third.append(copy)
    for copy in third:
        copy.wait_recv()
    o_ref[...] = whole[...]
    for copy in first + second + third:
        copy.wait_send()


def total_over_devices(parts):
    ccds, tiles = lax.axis_size("ccd"), lax.axis_size("tile")
    rows = parts.shape[1]
    dma = pltpu.SemaphoreType.DMA
    return pl.pallas_call(
        functools.partial(sum_kernel, ccds, tiles),
        out_shape=jax.ShapeDtypeStruct(parts.shape, jnp.float32),
        in_specs=[pl.BlockSpec(memory_space=pltpu.VMEM)],
        out_specs=pl.BlockSpec(memory_space=pltpu.VMEM),
        scratch_shapes=[
            pltpu.VMEM((tiles - 1, rows, LANES), jnp.float32),
            pltpu.VMEM((ccds, rows, LANES), jnp.float32),
            pltpu.VMEM((tiles, rows, LANES), jnp.float32),
            dma((tiles - 1,)), dma((tiles - 1,)),
            dma((ccds - 1,)), dma((ccds - 1,)),
            dma((tiles - 1,)), dma((tiles - 1,)),
        ],
        compiler_params=pltpu.CompilerParams(collective_id=0, has_side_effects=True),
    )(parts)


def matmul(a, b, contract=(1, 0)):
    return lax.dot_general(
        a, b, (((contract[0],), (contract[1],)), ((), ())), precision=HIGH, preferred_element_type=jnp.float32
    )


def factor_block(block, rows_ref):
    groups = LANES // 8
    full = (8, LANES)
    live = [block[8 * g:8 * g + 8, :] for g in range(groups)]
    lane = lax.broadcasted_iota(jnp.int32, full, 1)
    for g in range(groups):
        base = 8 * g
        inside = jnp.logical_and(lane >= base, lane < base + 8)
        cols = [jnp.broadcast_to(live[g][:, base + k:base + k + 1], full) for k in range(8)]
        small = {(j, k): jnp.broadcast_to(cols[k][j:j + 1, :], full) for j in range(8) for k in range(j, 8)}
        rows = []
        for k in range(8):
            row = jnp.broadcast_to(live[g][k:k + 1, :], full)
            rows.append(jnp.where(inside, jnp.where(lane == base + k, 1.0, 0.0), row))
        inv, lower = [], {}
        for j in range(8):
            inv.append(1.0 / small[j, j])
            for k in range(j + 1, 8):
                for m in range(k, 8):
                    small[k, m] = small[k, m] - (small[j, k] * small[j, m]) * inv[j]
            for k in range(j + 1, 8):
                lower[k, j] = small[j, k] * inv[j]
                rows[k] = rows[k] - lower[k, j] * rows[j]
        for j in range(8):
            pivot = small[j, j]
            root = lax.rsqrt(pivot)
            root = root * (1.5 - 0.5 * pivot * root * root)
            out = rows[j]
            for m in range(j, 8):
                out = jnp.where(lane == base + m, small[j, m], out)
            rows_ref[base + j:base + j + 1, :] = (out * root)[:1, :]
        if g == groups - 1:
            break
        back = [rows[k] * inv[k] for k in range(8)]
        for k in range(7, -1, -1):
            for m in range(k):
                back[m] = back[m] - lower[k, m] * back[k]
        for i in range(g + 1, groups):
            total = None
            for k in range(8):
                term = jnp.broadcast_to(live[i][:, base + k:base + k + 1], full) * back[k]
                total = term if total is None else total + term
            live[i] = jnp.where(inside, 0.0, live[i]) - total
    done = rows_ref[...]
    row_id = lax.broadcasted_iota(jnp.int32, (LANES, LANES), 0)
    col_id = lax.broadcasted_iota(jnp.int32, (LANES, LANES), 1)
    upper = jnp.where(col_id >= row_id, done, 0.0)
    inverse = jnp.where(col_id < row_id, done, jnp.where(col_id == row_id, 1.0 / done, 0.0))
    return upper, inverse


def split(value):
    high = value.astype(jnp.bfloat16)
    return high, (value - high.astype(jnp.float32)).astype(jnp.bfloat16)


def product(a, b, contract):
    return lax.dot_general(
        a, b, (((contract[0],), (contract[1],)), ((), ())), preferred_element_type=jnp.float32
    )


def smooth_rows(read, rows):
    decay = math.exp(-1.0 / 6.0)
    tail = math.exp(-(REACH + 1) / 6.0)
    ahead = read(0)
    for p in range(1, REACH + 1):
        ahead = ahead * decay + read(p)
    out = [ahead]
    for i in range(1, rows):
        ahead = ahead * decay + (read(REACH + i) - tail * read(i - 1))
        out.append(ahead)
    last = REACH + rows - 1
    back = read(last + REACH) * decay
    for k in range(REACH - 1, 0, -1):
        back = (back + read(last + k)) * decay
    out[rows - 1] = out[rows - 1] + back
    for i in range(rows - 2, -1, -1):
        p = REACH + i
        back = (back + read(p + 1)) * decay - tail * read(p + REACH + 1)
        out[i] = out[i] + back
    return out


def smooth_kernel(tile_rows, before_ref, own_ref, after_ref, w_ref, hi_ref, lo_ref, g_ref, pad, done):
    pad[0] = before_ref[...].astype(jnp.float32)
    pad[1] = own_ref[...].astype(jnp.float32)
    pad[2] = after_ref[...].astype(jnp.float32)
    exposures = hi_ref.shape[0]
    step = 32

    @pl.loop(0, exposures // step)
    def _(c):
        def read(p):
            return pad[p // tile_rows, pl.ds(c * (step * tile_rows) + p % tile_rows, step, stride=tile_rows), :]

        here = pl.multiple_of(c * step, step)
        for r, value in enumerate(smooth_rows(read, tile_rows)):
            done[r, pl.ds(here, step), :] = value

    for r in range(tile_rows):
        hi, lo = split(matmul(done[r], w_ref[...]))
        hi_ref[:, r * LANES:(r + 1) * LANES] = hi
        lo_ref[:, r * LANES:(r + 1) * LANES] = lo
    h = LANES
    cross = product(hi_ref[...], lo_ref[...], (1, 1))
    gram = product(hi_ref[...], hi_ref[...], (1, 1)) + product(lo_ref[...], lo_ref[...], (1, 1))
    gram = gram + (cross + cross.T)
    g_ref[0] = gram[:h, :h]
    g_ref[1] = gram[h:, :h]
    g_ref[2] = gram[h:, h:]


def smooth(before, own, after, weights, tile_rows):
    exposures = own.shape[0] // tile_rows
    pixels = tile_rows * LANES
    vm = pl.BlockSpec(memory_space=pltpu.VMEM)
    return pl.pallas_call(
        functools.partial(smooth_kernel, tile_rows),
        out_shape=(
            jax.ShapeDtypeStruct((exposures, pixels), jnp.bfloat16),
            jax.ShapeDtypeStruct((exposures, pixels), jnp.bfloat16),
            jax.ShapeDtypeStruct((3, LANES, LANES), jnp.float32),
        ),
        in_specs=[vm] * 4,
        out_specs=(vm,) * 3,
        scratch_shapes=[
            pltpu.VMEM((3,) + own.shape, jnp.float32),
            pltpu.VMEM((tile_rows, exposures, LANES), jnp.float32),
        ],
    )(before, own, after, weights)


def solve_kernel(pixel_total, g_ref, hi_ref, lo_ref, f_ref, b_ref, rows_ref, xh_ref, xl_ref, out32):
    h = LANES
    scale = 1.0 / pixel_total
    upper, inv1 = factor_block(g_ref[0] * scale, rows_ref)
    f_ref[:h, :h] = upper
    f_ref[h:, :h] = jnp.zeros((h, h), jnp.float32)
    low = matmul(g_ref[1] * scale, inv1, (1, 1))
    f_ref[:h, h:] = low.T
    rest = g_ref[2] * scale - matmul(low, low, (1, 1))
    upper, inv2 = factor_block(rest, rows_ref)
    f_ref[h:, h:] = upper
    xh_ref[:h, :h], xl_ref[:h, :h] = split(inv1)
    xh_ref[:h, h:] = jnp.zeros((h, h), jnp.bfloat16)
    xl_ref[:h, h:] = jnp.zeros((h, h), jnp.bfloat16)
    xh_ref[h:, h:], xl_ref[h:, h:] = split(inv2)
    xh_ref[h:, :h], xl_ref[h:, :h] = split(-matmul(inv2, matmul(low, inv1)))
    exposures, pixels = hi_ref.shape
    tile_rows = pixels // LANES
    for k in range(tile_rows // 2):
        at = slice(2 * k * LANES, 2 * (k + 1) * LANES)
        hi, lo = hi_ref[:, at], lo_ref[:, at]
        part = product(xh_ref[...], hi, (1, 0)) + (
            product(xh_ref[...], lo, (1, 0)) + product(xl_ref[...], hi, (1, 0)) + product(xl_ref[...], lo, (1, 0)))
        for i in range(2):
            out32[pl.ds(2 * k + i, exposures, stride=tile_rows), :] = part[:, i * LANES:(i + 1) * LANES]
    b_ref[...] = out32[...].astype(jnp.bfloat16)


def solve(gram, hi, lo, pixel_total):
    exposures, pixels = hi.shape
    vm = pl.BlockSpec(memory_space=pltpu.VMEM)
    return pl.pallas_call(
        functools.partial(solve_kernel, pixel_total),
        out_shape=(
            jax.ShapeDtypeStruct((exposures, exposures), jnp.float32),
            jax.ShapeDtypeStruct((exposures * pixels // LANES, LANES), jnp.bfloat16),
        ),
        in_specs=[vm, vm, vm],
        out_specs=(vm, vm),
        scratch_shapes=[
            pltpu.VMEM((LANES, LANES), jnp.float32),
            pltpu.VMEM((exposures, exposures), jnp.bfloat16),
            pltpu.VMEM((exposures, exposures), jnp.bfloat16),
            pltpu.VMEM((exposures * pixels // LANES, LANES), jnp.float32),
        ],
    )(gram, hi, lo)


def shift_rows(masked, axes):
    peers = lax.axis_size(axes)
    up = [(i, (i + 1) % peers) for i in range(peers - 1)]
    down = [(j, i) for i, j in up]
    return lax.ppermute(masked, axes, up), lax.ppermute(masked, axes, down)


def per_device(frames, source_mask, good_pixels):
    exposures, tile_rows, tile_cols = frames.shape
    masked = frames * source_mask.astype(jnp.bfloat16) * good_pixels.astype(jnp.bfloat16)[None]
    masked = masked.reshape(exposures * tile_rows, tile_cols)
    before, after = shift_rows(masked, ("ccd", "tile"))
    tiles = lax.axis_size("tile")
    pixel_total = float(tile_rows * tile_cols * lax.axis_size("ccd") * tiles)
    hi, lo, packed = smooth(before, masked, after, column_matrix(tile_cols), tile_rows)
    summed = total_over_devices(packed.reshape(tiles, 3 * LANES // tiles, LANES))
    factor, basis = solve(summed.reshape(3, LANES, LANES), hi, lo, pixel_total)
    return (factor, basis.reshape(exposures, tile_rows, tile_cols))


def solution(mesh):
    in_specs = (
        P(None, ("ccd", "tile"), None),
        P(None, ("ccd", "tile"), None),
        P(("ccd", "tile"), None),
    )
    out_specs = (P(), P(None, ("ccd", "tile"), None))
    return jax.shard_map(
        per_device, mesh=mesh, in_specs=in_specs, out_specs=out_specs, check_vma=False
    )
```

```python
import functools
import math

import jax
import jax.numpy as jnp
from jax import lax
from jax.experimental import pallas as pl
from jax.experimental.pallas import tpu as pltpu
from jax.sharding import PartitionSpec as P

REACH = 16
MESH = pl.DeviceIdType.MESH
HIGH = lax.Precision.HIGHEST
LANES = 128


def tap_weight(distance):
    offsets = jnp.arange(-REACH, REACH + 1).astype(jnp.float32)
    norm_sum = jnp.sqrt(jnp.sum(jnp.exp(-2.0 * jnp.abs(offsets) / 6.0)))
    inside = jnp.abs(distance) <= REACH
    return jnp.where(inside, jnp.exp(-jnp.abs(distance).astype(jnp.float32) / 6.0) / norm_sum, 0.0)


def column_matrix(tile_cols):
    in_cols = jnp.arange(tile_cols).reshape(tile_cols, 1)
    out_cols = jnp.arange(tile_cols).reshape(1, tile_cols)
    weights = tap_weight(in_cols - out_cols)
    offsets = jnp.arange(-REACH, REACH + 1).astype(jnp.float32)
    return weights / jnp.sqrt(jnp.sum(jnp.exp(-2.0 * jnp.abs(offsets) / 6.0)))


def matmul(a, b, contract=(1, 0)):
    return lax.dot_general(
        a, b, (((contract[0],), (contract[1],)), ((), ())), precision=HIGH, preferred_element_type=jnp.float32
    )


def factor_block(block, rows_ref):
    groups = LANES // 8
    full = (8, LANES)
    live = [block[8 * g:8 * g + 8, :] for g in range(groups)]
    lane = lax.broadcasted_iota(jnp.int32, full, 1)
    for g in range(groups):
        base = 8 * g
        inside = jnp.logical_and(lane >= base, lane < base + 8)
        cols = [jnp.broadcast_to(live[g][:, base + k:base + k + 1], full) for k in range(8)]
        small = {(j, k): jnp.broadcast_to(cols[k][j:j + 1, :], full) for j in range(8) for k in range(j, 8)}
        rows = []
        for k in range(8):
            row = jnp.broadcast_to(live[g][k:k + 1, :], full)
            rows.append(jnp.where(inside, jnp.where(lane == base + k, 1.0, 0.0), row))
        inv, lower = [], {}
        for j in range(8):
            inv.append(1.0 / small[j, j])
            for k in range(j + 1, 8):
                for m in range(k, 8):
                    small[k, m] = small[k, m] - (small[j, k] * small[j, m]) * inv[j]
            for k in range(j + 1, 8):
                lower[k, j] = small[j, k] * inv[j]
                rows[k] = rows[k] - lower[k, j] * rows[j]
        for j in range(8):
            pivot = small[j, j]
            root = lax.rsqrt(pivot)
            root = root * (1.5 - 0.5 * pivot * root * root)
            out = rows[j]
            for m in range(j, 8):
                out = jnp.where(lane == base + m, small[j, m], out)
            rows_ref[base + j:base + j + 1, :] = (out * root)[:1, :]
        if g == groups - 1:
            break
        back = [rows[k] * inv[k] for k in range(8)]
        for k in range(7, -1, -1):
            for m in range(k):
                back[m] = back[m] - lower[k, m] * back[k]
        for i in range(g + 1, groups):
            total = None
            for k in range(8):
                term = jnp.broadcast_to(live[i][:, base + k:base + k + 1], full) * back[k]
                total = term if total is None else total + term
            live[i] = jnp.where(inside, 0.0, live[i]) - total
    done = rows_ref[...]
    row_id = lax.broadcasted_iota(jnp.int32, (LANES, LANES), 0)
    col_id = lax.broadcasted_iota(jnp.int32, (LANES, LANES), 1)
    upper = jnp.where(col_id >= row_id, done, 0.0)
    inverse = jnp.where(col_id < row_id, done, jnp.where(col_id == row_id, 1.0 / done, 0.0))
    return upper, inverse


def split(value):
    high = value.astype(jnp.bfloat16)
    return high, (value - high.astype(jnp.float32)).astype(jnp.bfloat16)


def product(a, b, contract):
    return lax.dot_general(
        a, b, (((contract[0],), (contract[1],)), ((), ())), preferred_element_type=jnp.float32
    )


def smooth_rows(read, rows):
    decay = math.exp(-1.0 / 6.0)
    tail = math.exp(-(REACH + 1) / 6.0)
    ahead = read(0)
    for p in range(1, REACH + 1):
        ahead = ahead * decay + read(p)
    out = [ahead]
    for i in range(1, rows):
        ahead = ahead * decay + (read(REACH + i) - tail * read(i - 1))
        out.append(ahead)
    last = REACH + rows - 1
    back = read(last + REACH) * decay
    for k in range(REACH - 1, 0, -1):
        back = (back + read(last + k)) * decay
    out[rows - 1] = out[rows - 1] + back
    for i in range(rows - 2, -1, -1):
        p = REACH + i
        back = (back + read(p + 1)) * decay - tail * read(p + REACH + 1)
        out[i] = out[i] + back
    return out


CHUNKS = 4


def exchange_kernel(ccds, tiles, tile_rows, own_ref, w_ref, hi_ref, lo_ref, o_ref, halo, pad, done, mine,
                    near, far, whole, hs, hr, s1, r1, s2, r2, s3, r3):
    c, t = lax.axis_index("ccd"), lax.axis_index("tile")
    me, total = c * tiles + t, ccds * tiles
    after, before = lax.rem(me + 1, total), lax.rem(me + total - 1, total)
    after_id = (lax.div(after, tiles), lax.rem(after, tiles))
    before_id = (lax.div(before, tiles), lax.rem(before, tiles))
    barrier = pltpu.get_barrier_semaphore()
    for peer in (before_id, after_id):
        pl.semaphore_signal(barrier, inc=1, device_id=peer, device_id_type=MESH)
    for d in range(1, tiles):
        pl.semaphore_signal(barrier, inc=1, device_id=(c, lax.rem(t + d, tiles)), device_id_type=MESH)
    for d in range(1, ccds):
        pl.semaphore_signal(barrier, inc=1, device_id=(lax.rem(c + d, ccds), t), device_id_type=MESH)
    pl.semaphore_wait(barrier, tiles + ccds)
    exposures = hi_ref.shape[0]
    part = exposures // CHUNKS
    span = part * tile_rows
    moves = []
    for k in range(CHUNKS):
        rows = pl.ds(k * span, span)
        pair = []
        for side, peer in enumerate((after_id, before_id)):
            copy = pltpu.make_async_remote_copy(
                src_ref=own_ref.at[rows], dst_ref=halo.at[side, rows], send_sem=hs.at[side, k],
                recv_sem=hr.at[side, k], device_id=peer, device_id_type=MESH)
            copy.start()
            pair.append(copy)
        moves.append(pair)
    has_before = jnp.where(me > 0, 1.0, 0.0)
    has_after = jnp.where(me < total - 1, 1.0, 0.0)
    weights = w_ref[...]
    h = LANES
    for k in range(CHUNKS):
        rows = pl.ds(k * span, span)
        pad[1] = own_ref[rows, :].astype(jnp.float32)
        for copy in moves[k]:
            copy.wait_recv()
        pad[0] = halo[0, rows, :].astype(jnp.float32) * has_before
        pad[2] = halo[1, rows, :].astype(jnp.float32) * has_after
        step = 32

        @pl.loop(0, part // step)
        def _(n):
            def read(p):
                first = n * (step * tile_rows) + p % tile_rows
                return pad[p // tile_rows, pl.ds(first, step, stride=tile_rows), :]

            for r, value in enumerate(smooth_rows(read, tile_rows)):
                done[pl.ds(pl.multiple_of(r * part + n * step, step), step), :] = value

        hi, lo = split(matmul(done[...], weights))
        for r in range(tile_rows):
            hi_ref[k * part:(k + 1) * part, r * h:(r + 1) * h] = hi[r * part:(r + 1) * part]
            lo_ref[k * part:(k + 1) * part, r * h:(r + 1) * h] = lo[r * part:(r + 1) * part]
        if (k + 1) * part == h:
            hi, lo = hi_ref[:h, :], lo_ref[:h, :]
            cross = product(hi, lo, (1, 1))
            first = product(hi, hi, (1, 1)) + product(lo, lo, (1, 1)) + (cross + cross.T)
    hi, lo = hi_ref[h:, :], lo_ref[h:, :]
    rest = product(hi, hi_ref[...], (1, 1)) + product(lo, lo_ref[...], (1, 1)) + (
        product(hi, lo_ref[...], (1, 1)) + product(lo, hi_ref[...], (1, 1)))
    packed = jnp.concatenate([first, rest[:, :h], rest[:, h:]], axis=0)
    share = mine.shape[1]
    for i in range(tiles):
        mine[i] = packed[i * share:(i + 1) * share]
    sent = []
    for d in range(1, tiles):
        peer = lax.rem(t + d, tiles)
        copy = pltpu.make_async_remote_copy(
            src_ref=mine.at[peer], dst_ref=near.at[d - 1], send_sem=s1.at[d - 1], recv_sem=r1.at[d - 1],
            device_id=(c, peer), device_id_type=MESH)
        copy.start()
        sent.append(copy)
    value = mine[t]
    for d in range(1, tiles):
        sent[d - 1].wait_recv()
        value = value + near[d - 1]
    far[c] = value
    second = []
    for d in range(1, ccds):
        copy = pltpu.make_async_remote_copy(
            src_ref=far.at[c], dst_ref=far.at[c], send_sem=s2.at[d - 1], recv_sem=r2.at[d - 1],
            device_id=(lax.rem(c + d, ccds), t), device_id_type=MESH)
        copy.start()
        second.append(copy)
    for copy in second:
        copy.wait_recv()
    value = far[0]
    for i in range(1, ccds):
        value = value + far[i]
    whole[t] = value
    third = []
    for d in range(1, tiles):
        copy = pltpu.make_async_remote_copy(
            src_ref=whole.at[t], dst_ref=whole.at[t], send_sem=s3.at[d - 1], recv_sem=r3.at[d - 1],
            device_id=(c, lax.rem(t + d, tiles)), device_id_type=MESH)
        copy.start()
        third.append(copy)
    for copy in third:
        copy.wait_recv()
    o_ref[...] = whole[...]
    for copy in sum(moves, []) + sent + second + third:
        copy.wait_send()


def exchange(masked, weights, tile_rows):
    ccds, tiles = lax.axis_size("ccd"), lax.axis_size("tile")
    exposures = masked.shape[0] // tile_rows
    pixels = tile_rows * LANES
    share = 3 * LANES // tiles
    dma = pltpu.SemaphoreType.DMA
    vm = pl.BlockSpec(memory_space=pltpu.VMEM)
    split_shape = jax.ShapeDtypeStruct((exposures, pixels), jnp.bfloat16)
    span = masked.shape[0] // CHUNKS
    return pl.pallas_call(
        functools.partial(exchange_kernel, ccds, tiles, tile_rows),
        out_shape=(split_shape, split_shape, jax.ShapeDtypeStruct((tiles, share, LANES), jnp.float32)),
        in_specs=[vm, vm],
        out_specs=(vm,) * 3,
        scratch_shapes=[
            pltpu.VMEM((2,) + masked.shape, jnp.bfloat16),
            pltpu.VMEM((3, span, LANES), jnp.float32),
            pltpu.VMEM((span, LANES), jnp.float32),
            pltpu.VMEM((tiles, share, LANES), jnp.float32),
            pltpu.VMEM((tiles - 1, share, LANES), jnp.float32),
            pltpu.VMEM((ccds, share, LANES), jnp.float32),
            pltpu.VMEM((tiles, share, LANES), jnp.float32),
            dma((2, CHUNKS)), dma((2, CHUNKS)),
            dma((tiles - 1,)), dma((tiles - 1,)),
            dma((ccds - 1,)), dma((ccds - 1,)),
            dma((tiles - 1,)), dma((tiles - 1,)),
        ],
        compiler_params=pltpu.CompilerParams(collective_id=0, has_side_effects=True),
    )(masked, weights)


def solve_kernel(pixel_total, g_ref, hi_ref, lo_ref, f_ref, b_ref, rows_ref, xh_ref, xl_ref, out32):
    h = LANES
    scale = 1.0 / pixel_total
    upper, inv1 = factor_block(g_ref[0] * scale, rows_ref)
    f_ref[:h, :h] = upper
    f_ref[h:, :h] = jnp.zeros((h, h), jnp.float32)
    low = matmul(g_ref[1] * scale, inv1, (1, 1))
    f_ref[:h, h:] = low.T
    rest = g_ref[2] * scale - matmul(low, low, (1, 1))
    upper, inv2 = factor_block(rest, rows_ref)
    f_ref[h:, h:] = upper
    xh_ref[:h, :h], xl_ref[:h, :h] = split(inv1)
    xh_ref[:h, h:] = jnp.zeros((h, h), jnp.bfloat16)
    xl_ref[:h, h:] = jnp.zeros((h, h), jnp.bfloat16)
    xh_ref[h:, h:], xl_ref[h:, h:] = split(inv2)
    xh_ref[h:, :h], xl_ref[h:, :h] = split(-matmul(inv2, matmul(low, inv1)))
    exposures, pixels = hi_ref.shape
    tile_rows = pixels // LANES
    for k in range(tile_rows // 2):
        at = slice(2 * k * LANES, 2 * (k + 1) * LANES)
        hi, lo = hi_ref[:, at], lo_ref[:, at]
        part = product(xh_ref[...], hi, (1, 0)) + (
            product(xh_ref[...], lo, (1, 0)) + product(xl_ref[...], hi, (1, 0)) + product(xl_ref[...], lo, (1, 0)))
        for i in range(2):
            out32[pl.ds(2 * k + i, exposures, stride=tile_rows), :] = part[:, i * LANES:(i + 1) * LANES]
    b_ref[...] = out32[...].astype(jnp.bfloat16)


def solve(gram, hi, lo, pixel_total):
    exposures, pixels = hi.shape
    vm = pl.BlockSpec(memory_space=pltpu.VMEM)
    return pl.pallas_call(
        functools.partial(solve_kernel, pixel_total),
        out_shape=(
            jax.ShapeDtypeStruct((exposures, exposures), jnp.float32),
            jax.ShapeDtypeStruct((exposures * pixels // LANES, LANES), jnp.bfloat16),
        ),
        in_specs=[vm, vm, vm],
        out_specs=(vm, vm),
        scratch_shapes=[
            pltpu.VMEM((LANES, LANES), jnp.float32),
            pltpu.VMEM((exposures, exposures), jnp.bfloat16),
            pltpu.VMEM((exposures, exposures), jnp.bfloat16),
            pltpu.VMEM((exposures * pixels // LANES, LANES), jnp.float32),
        ],
    )(gram, hi, lo)


def per_device(frames, source_mask, good_pixels):
    exposures, tile_rows, tile_cols = frames.shape
    masked = frames * source_mask.astype(jnp.bfloat16) * good_pixels.astype(jnp.bfloat16)[None]
    masked = masked.reshape(exposures * tile_rows, tile_cols)
    tiles = lax.axis_size("tile")
    pixel_total = float(tile_rows * tile_cols * lax.axis_size("ccd") * tiles)
    hi, lo, summed = exchange(masked, column_matrix(tile_cols), tile_rows)
    factor, basis = solve(summed.reshape(3, LANES, LANES), hi, lo, pixel_total)
    return (factor, basis.reshape(exposures, tile_rows, tile_cols))


def solution(mesh):
    in_specs = (
        P(None, ("ccd", "tile"), None),
        P(None, ("ccd", "tile"), None),
        P(("ccd", "tile"), None),
    )
    out_specs = (P(), P(None, ("ccd", "tile"), None))
    return jax.shard_map(
        per_device, mesh=mesh, in_specs=in_specs, out_specs=out_specs, check_vma=False
    )
```

```python
import functools
import math

import jax
import jax.numpy as jnp
import numpy as np
from jax import lax
from jax.experimental import pallas as pl
from jax.experimental.pallas import tpu as pltpu
from jax.sharding import PartitionSpec as P

REACH = 16
MESH = pl.DeviceIdType.MESH
HIGH = lax.Precision.HIGHEST
LANES = 128


def column_matrix(tile_cols):
    distance = np.abs(np.arange(tile_cols)[:, None] - np.arange(tile_cols)[None, :])
    norm = np.sum(np.exp(-2.0 * np.abs(np.arange(-REACH, REACH + 1)) / 6.0))
    return np.where(distance <= REACH, np.exp(-distance / 6.0) / norm, 0.0).astype(np.float32)


def matmul(a, b, contract=(1, 0)):
    return lax.dot_general(
        a, b, (((contract[0],), (contract[1],)), ((), ())), precision=HIGH, preferred_element_type=jnp.float32
    )


def factor_block(block, rows_ref):
    groups = LANES // 8
    full = (8, LANES)
    live = [block[8 * g:8 * g + 8, :] for g in range(groups)]
    lane = lax.broadcasted_iota(jnp.int32, full, 1)
    for g in range(groups):
        base = 8 * g
        inside = jnp.logical_and(lane >= base, lane < base + 8)
        cols = [jnp.broadcast_to(live[g][:, base + k:base + k + 1], full) for k in range(8)]
        small = {(j, k): jnp.broadcast_to(cols[k][j:j + 1, :], full) for j in range(8) for k in range(j, 8)}
        rows = []
        for k in range(8):
            row = jnp.broadcast_to(live[g][k:k + 1, :], full)
            rows.append(jnp.where(inside, jnp.where(lane == base + k, 1.0, 0.0), row))
        inv, lower = [], {}
        for j in range(8):
            inv.append(1.0 / small[j, j])
            for k in range(j + 1, 8):
                for m in range(k, 8):
                    small[k, m] = small[k, m] - (small[j, k] * small[j, m]) * inv[j]
            for k in range(j + 1, 8):
                lower[k, j] = small[j, k] * inv[j]
                rows[k] = rows[k] - lower[k, j] * rows[j]
        for j in range(8):
            pivot = small[j, j]
            root = lax.rsqrt(pivot)
            root = root * (1.5 - 0.5 * pivot * root * root)
            out = rows[j]
            for m in range(j, 8):
                out = jnp.where(lane == base + m, small[j, m], out)
            rows_ref[base + j:base + j + 1, :] = (out * root)[:1, :]
        if g == groups - 1:
            break
        back = [rows[k] * inv[k] for k in range(8)]
        for k in range(7, -1, -1):
            for m in range(k):
                back[m] = back[m] - lower[k, m] * back[k]
        for i in range(g + 1, groups):
            total = None
            for k in range(8):
                term = jnp.broadcast_to(live[i][:, base + k:base + k + 1], full) * back[k]
                total = term if total is None else total + term
            live[i] = jnp.where(inside, 0.0, live[i]) - total
    done = rows_ref[...]
    row_id = lax.broadcasted_iota(jnp.int32, (LANES, LANES), 0)
    col_id = lax.broadcasted_iota(jnp.int32, (LANES, LANES), 1)
    upper = jnp.where(col_id >= row_id, done, 0.0)
    inverse = jnp.where(col_id < row_id, done, jnp.where(col_id == row_id, 1.0 / done, 0.0))
    return upper, inverse


def split(value):
    high = value.astype(jnp.bfloat16)
    return high, (value - high.astype(jnp.float32)).astype(jnp.bfloat16)


def product(a, b, contract):
    return lax.dot_general(
        a, b, (((contract[0],), (contract[1],)), ((), ())), preferred_element_type=jnp.float32
    )


def smooth_rows(read, rows):
    decay = math.exp(-1.0 / 6.0)
    tail = math.exp(-(REACH + 1) / 6.0)
    ahead = read(0)
    for p in range(1, REACH + 1):
        ahead = ahead * decay + read(p)
    out = [ahead]
    for i in range(1, rows):
        ahead = ahead * decay + (read(REACH + i) - tail * read(i - 1))
        out.append(ahead)
    last = REACH + rows - 1
    back = read(last + REACH) * decay
    for k in range(REACH - 1, 0, -1):
        back = (back + read(last + k)) * decay
    out[rows - 1] = out[rows - 1] + back
    for i in range(rows - 2, -1, -1):
        p = REACH + i
        back = (back + read(p + 1)) * decay - tail * read(p + REACH + 1)
        out[i] = out[i] + back
    return out


CHUNKS = 4


def exchange_kernel(ccds, tiles, tile_rows, frame_ref, mask_ref, good_ref, w_ref, hi_ref, lo_ref, o_ref, own_ref, halo, pad, done, mine,
                    near, far, whole, hs, hr, s1, r1, s2, r2, s3, r3):
    c, t = lax.axis_index("ccd"), lax.axis_index("tile")
    me, total = c * tiles + t, ccds * tiles
    after, before = lax.rem(me + 1, total), lax.rem(me + total - 1, total)
    after_id = (lax.div(after, tiles), lax.rem(after, tiles))
    before_id = (lax.div(before, tiles), lax.rem(before, tiles))
    barrier = pltpu.get_barrier_semaphore()
    good = good_ref[...].astype(jnp.float32)[None]
    for peer in (before_id, after_id):
        pl.semaphore_signal(barrier, inc=1, device_id=peer, device_id_type=MESH)
    for d in range(1, tiles):
        pl.semaphore_signal(barrier, inc=1, device_id=(c, lax.rem(t + d, tiles)), device_id_type=MESH)
    for d in range(1, ccds):
        pl.semaphore_signal(barrier, inc=1, device_id=(lax.rem(c + d, ccds), t), device_id_type=MESH)
    exposures = hi_ref.shape[0]
    part = exposures // CHUNKS
    span = part * tile_rows
    moves = []
    for k in range(CHUNKS):
        rows = pl.ds(k * span, span)
        block = pl.ds(k * part, part)
        value = frame_ref[block].astype(jnp.float32) * (mask_ref[block].astype(jnp.float32) * good)
        own_ref[rows, :] = value.astype(jnp.bfloat16).reshape(span, LANES)
        if k == 0:
            pl.semaphore_wait(barrier, tiles + ccds)
        pair = []
        for side, peer in enumerate((after_id, before_id)):
            copy = pltpu.make_async_remote_copy(
                src_ref=own_ref.at[rows], dst_ref=halo.at[side, rows], send_sem=hs.at[side, k],
                recv_sem=hr.at[side, k], device_id=peer, device_id_type=MESH)
            copy.start()
            pair.append(copy)
        moves.append(pair)
    has_before = jnp.where(me > 0, 1.0, 0.0)
    has_after = jnp.where(me < total - 1, 1.0, 0.0)
    weights = w_ref[...]
    h = LANES
    for k in range(CHUNKS):
        rows = pl.ds(k * span, span)
        pad[1] = own_ref[rows, :].astype(jnp.float32)
        for copy in moves[k]:
            copy.wait_recv()
        pad[0] = halo[0, rows, :].astype(jnp.float32) * has_before
        pad[2] = halo[1, rows, :].astype(jnp.float32) * has_after
        step = 32

        @pl.loop(0, part // step)
        def _(n):
            def read(p):
                first = n * (step * tile_rows) + p % tile_rows
                return pad[p // tile_rows, pl.ds(first, step, stride=tile_rows), :]

            for r, value in enumerate(smooth_rows(read, tile_rows)):
                done[pl.ds(pl.multiple_of(r * part + n * step, step), step), :] = value

        hi, lo = split(matmul(done[...], weights))
        for r in range(tile_rows):
            hi_ref[k * part:(k + 1) * part, r * h:(r + 1) * h] = hi[r * part:(r + 1) * part]
            lo_ref[k * part:(k + 1) * part, r * h:(r + 1) * h] = lo[r * part:(r + 1) * part]
        if (k + 1) * part == h:
            hi, lo = hi_ref[:h, :], lo_ref[:h, :]
            cross = product(hi, lo, (1, 1))
            first = product(hi, hi, (1, 1)) + product(lo, lo, (1, 1)) + (cross + cross.T)
    hi, lo = hi_ref[h:, :], lo_ref[h:, :]
    rest = product(hi, hi_ref[...], (1, 1)) + product(lo, lo_ref[...], (1, 1)) + (
        product(hi, lo_ref[...], (1, 1)) + product(lo, hi_ref[...], (1, 1)))
    packed = jnp.concatenate([first, rest[:, :h], rest[:, h:]], axis=0)
    share = mine.shape[1]
    for i in range(tiles):
        mine[i] = packed[i * share:(i + 1) * share]
    sent = []
    for d in range(1, tiles):
        peer = lax.rem(t + d, tiles)
        copy = pltpu.make_async_remote_copy(
            src_ref=mine.at[peer], dst_ref=near.at[d - 1], send_sem=s1.at[d - 1], recv_sem=r1.at[d - 1],
            device_id=(c, peer), device_id_type=MESH)
        copy.start()
        sent.append(copy)
    value = mine[t]
    for d in range(1, tiles):
        sent[d - 1].wait_recv()
        value = value + near[d - 1]
    far[c] = value
    second = []
    for d in range(1, ccds):
        copy = pltpu.make_async_remote_copy(
            src_ref=far.at[c], dst_ref=far.at[c], send_sem=s2.at[d - 1], recv_sem=r2.at[d - 1],
            device_id=(lax.rem(c + d, ccds), t), device_id_type=MESH)
        copy.start()
        second.append(copy)
    for copy in second:
        copy.wait_recv()
    value = far[0]
    for i in range(1, ccds):
        value = value + far[i]
    whole[t] = value
    third = []
    for d in range(1, tiles):
        copy = pltpu.make_async_remote_copy(
            src_ref=whole.at[t], dst_ref=whole.at[t], send_sem=s3.at[d - 1], recv_sem=r3.at[d - 1],
            device_id=(c, lax.rem(t + d, tiles)), device_id_type=MESH)
        copy.start()
        third.append(copy)
    for copy in third:
        copy.wait_recv()
    o_ref[...] = whole[...]
    for copy in sum(moves, []) + sent + second + third:
        copy.wait_send()


def exchange(frames, source_mask, good_pixels, weights):
    ccds, tiles = lax.axis_size("ccd"), lax.axis_size("tile")
    exposures, tile_rows, _ = frames.shape
    pixels = tile_rows * LANES
    share = 3 * LANES // tiles
    dma = pltpu.SemaphoreType.DMA
    vm = pl.BlockSpec(memory_space=pltpu.VMEM)
    split_shape = jax.ShapeDtypeStruct((exposures, pixels), jnp.bfloat16)
    span = exposures * tile_rows // CHUNKS
    return pl.pallas_call(
        functools.partial(exchange_kernel, ccds, tiles, tile_rows),
        out_shape=(split_shape, split_shape, jax.ShapeDtypeStruct((tiles, share, LANES), jnp.float32)),
        in_specs=[vm] * 4,
        out_specs=(vm,) * 3,
        scratch_shapes=[
            pltpu.VMEM((exposures * tile_rows, LANES), jnp.bfloat16),
            pltpu.VMEM((2, exposures * tile_rows, LANES), jnp.bfloat16),
            pltpu.VMEM((3, span, LANES), jnp.float32),
            pltpu.VMEM((span, LANES), jnp.float32),
            pltpu.VMEM((tiles, share, LANES), jnp.float32),
            pltpu.VMEM((tiles - 1, share, LANES), jnp.float32),
            pltpu.VMEM((ccds, share, LANES), jnp.float32),
            pltpu.VMEM((tiles, share, LANES), jnp.float32),
            dma((2, CHUNKS)), dma((2, CHUNKS)),
            dma((tiles - 1,)), dma((tiles - 1,)),
            dma((ccds - 1,)), dma((ccds - 1,)),
            dma((tiles - 1,)), dma((tiles - 1,)),
        ],
        compiler_params=pltpu.CompilerParams(collective_id=0, has_side_effects=True),
    )(frames, source_mask, good_pixels, weights)


def solve_kernel(pixel_total, g_ref, hi_ref, lo_ref, f_ref, b_ref, rows_ref, xh_ref, xl_ref, out32):
    h = LANES
    scale = 1.0 / pixel_total
    upper, inv1 = factor_block(g_ref[0] * scale, rows_ref)
    f_ref[:h, :h] = upper
    f_ref[h:, :h] = jnp.zeros((h, h), jnp.float32)
    low = matmul(g_ref[1] * scale, inv1, (1, 1))
    f_ref[:h, h:] = low.T
    rest = g_ref[2] * scale - matmul(low, low, (1, 1))
    upper, inv2 = factor_block(rest, rows_ref)
    f_ref[h:, h:] = upper
    xh_ref[:h, :h], xl_ref[:h, :h] = split(inv1)
    xh_ref[:h, h:] = jnp.zeros((h, h), jnp.bfloat16)
    xl_ref[:h, h:] = jnp.zeros((h, h), jnp.bfloat16)
    xh_ref[h:, h:], xl_ref[h:, h:] = split(inv2)
    xh_ref[h:, :h], xl_ref[h:, :h] = split(-matmul(inv2, matmul(low, inv1)))
    exposures, pixels = hi_ref.shape
    tile_rows = pixels // LANES
    for k in range(tile_rows // 2):
        at = slice(2 * k * LANES, 2 * (k + 1) * LANES)
        hi, lo = hi_ref[:, at], lo_ref[:, at]
        part = product(xh_ref[...], hi, (1, 0)) + (
            product(xh_ref[...], lo, (1, 0)) + product(xl_ref[...], hi, (1, 0)) + product(xl_ref[...], lo, (1, 0)))
        for i in range(2):
            out32[pl.ds(2 * k + i, exposures, stride=tile_rows), :] = part[:, i * LANES:(i + 1) * LANES]
    b_ref[...] = out32[...].astype(jnp.bfloat16)


def solve(gram, hi, lo, pixel_total):
    exposures, pixels = hi.shape
    vm = pl.BlockSpec(memory_space=pltpu.VMEM)
    return pl.pallas_call(
        functools.partial(solve_kernel, pixel_total),
        out_shape=(
            jax.ShapeDtypeStruct((exposures, exposures), jnp.float32),
            jax.ShapeDtypeStruct((exposures * pixels // LANES, LANES), jnp.bfloat16),
        ),
        in_specs=[vm, vm, vm],
        out_specs=(vm, vm),
        scratch_shapes=[
            pltpu.VMEM((LANES, LANES), jnp.float32),
            pltpu.VMEM((exposures, exposures), jnp.bfloat16),
            pltpu.VMEM((exposures, exposures), jnp.bfloat16),
            pltpu.VMEM((exposures * pixels // LANES, LANES), jnp.float32),
        ],
    )(gram, hi, lo)


def per_device(frames, source_mask, good_pixels):
    exposures, tile_rows, tile_cols = frames.shape
    tiles = lax.axis_size("tile")
    pixel_total = float(tile_rows * tile_cols * lax.axis_size("ccd") * tiles)
    hi, lo, summed = exchange(frames, source_mask, good_pixels, column_matrix(tile_cols))
    factor, basis = solve(summed.reshape(3, LANES, LANES), hi, lo, pixel_total)
    return (factor, basis.reshape(exposures, tile_rows, tile_cols))


def solution(mesh):
    in_specs = (
        P(None, ("ccd", "tile"), None),
        P(None, ("ccd", "tile"), None),
        P(("ccd", "tile"), None),
    )
    out_specs = (P(), P(None, ("ccd", "tile"), None))
    return jax.shard_map(
        per_device, mesh=mesh, in_specs=in_specs, out_specs=out_specs, check_vma=False
    )
```

```python
import functools
import math

import jax
import jax.numpy as jnp
import numpy as np
from jax import lax
from jax.experimental import pallas as pl
from jax.experimental.pallas import tpu as pltpu
from jax.sharding import PartitionSpec as P

REACH = 16
MESH = pl.DeviceIdType.MESH
HIGH = lax.Precision.HIGHEST
LANES = 128


def column_matrix(tile_cols):
    distance = np.abs(np.arange(tile_cols)[:, None] - np.arange(tile_cols)[None, :])
    norm = np.sum(np.exp(-2.0 * np.abs(np.arange(-REACH, REACH + 1)) / 6.0))
    return np.where(distance <= REACH, np.exp(-distance / 6.0) / norm, 0.0).astype(np.float32)


def matmul(a, b, contract=(1, 0)):
    return lax.dot_general(
        a, b, (((contract[0],), (contract[1],)), ((), ())), precision=HIGH, preferred_element_type=jnp.float32
    )


def factor_block(block, rows_ref):
    groups = LANES // 8
    full = (8, LANES)
    live = [block[8 * g:8 * g + 8, :] for g in range(groups)]
    lane = lax.broadcasted_iota(jnp.int32, full, 1)
    for g in range(groups):
        base = 8 * g
        inside = jnp.logical_and(lane >= base, lane < base + 8)
        cols = [jnp.broadcast_to(live[g][:, base + k:base + k + 1], full) for k in range(8)]
        small = {(j, k): jnp.broadcast_to(cols[k][j:j + 1, :], full) for j in range(8) for k in range(j, 8)}
        rows = []
        for k in range(8):
            row = jnp.broadcast_to(live[g][k:k + 1, :], full)
            rows.append(jnp.where(inside, jnp.where(lane == base + k, 1.0, 0.0), row))
        inv, lower = [], {}
        for j in range(8):
            inv.append(1.0 / small[j, j])
            for k in range(j + 1, 8):
                for m in range(k, 8):
                    small[k, m] = small[k, m] - (small[j, k] * small[j, m]) * inv[j]
            for k in range(j + 1, 8):
                lower[k, j] = small[j, k] * inv[j]
                rows[k] = rows[k] - lower[k, j] * rows[j]
        for j in range(8):
            pivot = small[j, j]
            root = lax.rsqrt(pivot)
            root = root * (1.5 - 0.5 * pivot * root * root)
            out = rows[j]
            for m in range(j, 8):
                out = jnp.where(lane == base + m, small[j, m], out)
            rows_ref[base + j:base + j + 1, :] = (out * root)[:1, :]
        if g == groups - 1:
            break
        back = [rows[k] * inv[k] for k in range(8)]
        for k in range(7, -1, -1):
            for m in range(k):
                back[m] = back[m] - lower[k, m] * back[k]
        for i in range(g + 1, groups):
            total = None
            for k in range(8):
                term = jnp.broadcast_to(live[i][:, base + k:base + k + 1], full) * back[k]
                total = term if total is None else total + term
            live[i] = jnp.where(inside, 0.0, live[i]) - total
    done = rows_ref[...]
    row_id = lax.broadcasted_iota(jnp.int32, (LANES, LANES), 0)
    col_id = lax.broadcasted_iota(jnp.int32, (LANES, LANES), 1)
    upper = jnp.where(col_id >= row_id, done, 0.0)
    inverse = jnp.where(col_id < row_id, done, jnp.where(col_id == row_id, 1.0 / done, 0.0))
    return upper, inverse


def split(value):
    high = value.astype(jnp.bfloat16)
    return high, (value - high.astype(jnp.float32)).astype(jnp.bfloat16)


def product(a, b, contract):
    return lax.dot_general(
        a, b, (((contract[0],), (contract[1],)), ((), ())), preferred_element_type=jnp.float32
    )


def smooth_rows(read, rows):
    decay = math.exp(-1.0 / 6.0)
    tail = math.exp(-(REACH + 1) / 6.0)
    ahead = read(0)
    for p in range(1, REACH + 1):
        ahead = ahead * decay + read(p)
    out = [ahead]
    for i in range(1, rows):
        ahead = ahead * decay + (read(REACH + i) - tail * read(i - 1))
        out.append(ahead)
    last = REACH + rows - 1
    back = read(last + REACH) * decay
    for k in range(REACH - 1, 0, -1):
        back = (back + read(last + k)) * decay
    out[rows - 1] = out[rows - 1] + back
    for i in range(rows - 2, -1, -1):
        p = REACH + i
        back = (back + read(p + 1)) * decay - tail * read(p + REACH + 1)
        out[i] = out[i] + back
    return out


CHUNKS = 8


def exchange_kernel(ccds, tiles, tile_rows, frame_ref, mask_ref, good_ref, w_ref, hi_ref, lo_ref, o_ref, own_ref, halo, pad, done, mine,
                    near, far, whole, hs, hr, s1, r1, s2, r2, s3, r3):
    c, t = lax.axis_index("ccd"), lax.axis_index("tile")
    me, total = c * tiles + t, ccds * tiles
    after, before = lax.rem(me + 1, total), lax.rem(me + total - 1, total)
    after_id = (lax.div(after, tiles), lax.rem(after, tiles))
    before_id = (lax.div(before, tiles), lax.rem(before, tiles))
    barrier = pltpu.get_barrier_semaphore()
    good = good_ref[...].astype(jnp.float32)[None]
    for peer in (before_id, after_id):
        pl.semaphore_signal(barrier, inc=1, device_id=peer, device_id_type=MESH)
    for d in range(1, tiles):
        pl.semaphore_signal(barrier, inc=1, device_id=(c, lax.rem(t + d, tiles)), device_id_type=MESH)
    for d in range(1, ccds):
        pl.semaphore_signal(barrier, inc=1, device_id=(lax.rem(c + d, ccds), t), device_id_type=MESH)
    exposures = hi_ref.shape[0]
    part = exposures // CHUNKS
    span = part * tile_rows
    moves = []
    for k in range(CHUNKS):
        rows = pl.ds(k * span, span)
        block = pl.ds(k * part, part)
        value = frame_ref[block].astype(jnp.float32) * (mask_ref[block].astype(jnp.float32) * good)
        own_ref[rows, :] = value.astype(jnp.bfloat16).reshape(span, LANES)
        if k == 0:
            pl.semaphore_wait(barrier, tiles + ccds)
        pair = []
        for side, peer in enumerate((after_id, before_id)):
            copy = pltpu.make_async_remote_copy(
                src_ref=own_ref.at[rows], dst_ref=halo.at[side, rows], send_sem=hs.at[side, k],
                recv_sem=hr.at[side, k], device_id=peer, device_id_type=MESH)
            copy.start()
            pair.append(copy)
        moves.append(pair)
    has_before = jnp.where(me > 0, 1.0, 0.0)
    has_after = jnp.where(me < total - 1, 1.0, 0.0)
    weights = w_ref[...]
    h = LANES
    for k in range(CHUNKS):
        rows = pl.ds(k * span, span)
        pad[1] = own_ref[rows, :].astype(jnp.float32)
        for copy in moves[k]:
            copy.wait_recv()
        pad[0] = halo[0, rows, :].astype(jnp.float32) * has_before
        pad[2] = halo[1, rows, :].astype(jnp.float32) * has_after
        step = 32

        @pl.loop(0, part // step)
        def _(n):
            def read(p):
                first = n * (step * tile_rows) + p % tile_rows
                return pad[p // tile_rows, pl.ds(first, step, stride=tile_rows), :]

            for r, value in enumerate(smooth_rows(read, tile_rows)):
                done[pl.ds(pl.multiple_of(r * part + n * step, step), step), :] = value

        hi, lo = split(matmul(done[...], weights))
        for r in range(tile_rows):
            hi_ref[k * part:(k + 1) * part, r * h:(r + 1) * h] = hi[r * part:(r + 1) * part]
            lo_ref[k * part:(k + 1) * part, r * h:(r + 1) * h] = lo[r * part:(r + 1) * part]
        if (k + 1) * part == h:
            hi, lo = hi_ref[:h, :], lo_ref[:h, :]
            cross = product(hi, lo, (1, 1))
            first = product(hi, hi, (1, 1)) + product(lo, lo, (1, 1)) + (cross + cross.T)
    hi, lo = hi_ref[h:, :], lo_ref[h:, :]
    rest = product(hi, hi_ref[...], (1, 1)) + product(lo, lo_ref[...], (1, 1)) + (
        product(hi, lo_ref[...], (1, 1)) + product(lo, hi_ref[...], (1, 1)))
    packed = jnp.concatenate([first, rest[:, :h], rest[:, h:]], axis=0)
    share = mine.shape[1]
    for i in range(tiles):
        mine[i] = packed[i * share:(i + 1) * share]
    sent = []
    for d in range(1, tiles):
        peer = lax.rem(t + d, tiles)
        copy = pltpu.make_async_remote_copy(
            src_ref=mine.at[peer], dst_ref=near.at[d - 1], send_sem=s1.at[d - 1], recv_sem=r1.at[d - 1],
            device_id=(c, peer), device_id_type=MESH)
        copy.start()
        sent.append(copy)
    value = mine[t]
    for d in range(1, tiles):
        sent[d - 1].wait_recv()
        value = value + near[d - 1]
    far[c] = value
    second = []
    for d in range(1, ccds):
        copy = pltpu.make_async_remote_copy(
            src_ref=far.at[c], dst_ref=far.at[c], send_sem=s2.at[d - 1], recv_sem=r2.at[d - 1],
            device_id=(lax.rem(c + d, ccds), t), device_id_type=MESH)
        copy.start()
        second.append(copy)
    for copy in second:
        copy.wait_recv()
    value = far[0]
    for i in range(1, ccds):
        value = value + far[i]
    whole[t] = value
    third = []
    for d in range(1, tiles):
        copy = pltpu.make_async_remote_copy(
            src_ref=whole.at[t], dst_ref=whole.at[t], send_sem=s3.at[d - 1], recv_sem=r3.at[d - 1],
            device_id=(c, lax.rem(t + d, tiles)), device_id_type=MESH)
        copy.start()
        third.append(copy)
    for copy in third:
        copy.wait_recv()
    o_ref[...] = whole[...]
    for copy in sum(moves, []) + sent + second + third:
        copy.wait_send()


def exchange(frames, source_mask, good_pixels, weights):
    ccds, tiles = lax.axis_size("ccd"), lax.axis_size("tile")
    exposures, tile_rows, _ = frames.shape
    pixels = tile_rows * LANES
    share = 3 * LANES // tiles
    dma = pltpu.SemaphoreType.DMA
    vm = pl.BlockSpec(memory_space=pltpu.VMEM)
    split_shape = jax.ShapeDtypeStruct((exposures, pixels), jnp.bfloat16)
    span = exposures * tile_rows // CHUNKS
    return pl.pallas_call(
        functools.partial(exchange_kernel, ccds, tiles, tile_rows),
        out_shape=(split_shape, split_shape, jax.ShapeDtypeStruct((tiles, share, LANES), jnp.float32)),
        in_specs=[vm] * 4,
        out_specs=(vm,) * 3,
        scratch_shapes=[
            pltpu.VMEM((exposures * tile_rows, LANES), jnp.bfloat16),
            pltpu.VMEM((2, exposures * tile_rows, LANES), jnp.bfloat16),
            pltpu.VMEM((3, span, LANES), jnp.float32),
            pltpu.VMEM((span, LANES), jnp.float32),
            pltpu.VMEM((tiles, share, LANES), jnp.float32),
            pltpu.VMEM((tiles - 1, share, LANES), jnp.float32),
            pltpu.VMEM((ccds, share, LANES), jnp.float32),
            pltpu.VMEM((tiles, share, LANES), jnp.float32),
            dma((2, CHUNKS)), dma((2, CHUNKS)),
            dma((tiles - 1,)), dma((tiles - 1,)),
            dma((ccds - 1,)), dma((ccds - 1,)),
            dma((tiles - 1,)), dma((tiles - 1,)),
        ],
        compiler_params=pltpu.CompilerParams(collective_id=0, has_side_effects=True),
    )(frames, source_mask, good_pixels, weights)


def solve_kernel(pixel_total, g_ref, hi_ref, lo_ref, f_ref, b_ref, rows_ref, xh_ref, xl_ref, out32):
    h = LANES
    scale = 1.0 / pixel_total
    upper, inv1 = factor_block(g_ref[0] * scale, rows_ref)
    f_ref[:h, :h] = upper
    f_ref[h:, :h] = jnp.zeros((h, h), jnp.float32)
    low = matmul(g_ref[1] * scale, inv1, (1, 1))
    f_ref[:h, h:] = low.T
    rest = g_ref[2] * scale - matmul(low, low, (1, 1))
    upper, inv2 = factor_block(rest, rows_ref)
    f_ref[h:, h:] = upper
    xh_ref[:h, :h], xl_ref[:h, :h] = split(inv1)
    xh_ref[:h, h:] = jnp.zeros((h, h), jnp.bfloat16)
    xl_ref[:h, h:] = jnp.zeros((h, h), jnp.bfloat16)
    xh_ref[h:, h:], xl_ref[h:, h:] = split(inv2)
    xh_ref[h:, :h], xl_ref[h:, :h] = split(-matmul(inv2, matmul(low, inv1)))
    exposures, pixels = hi_ref.shape
    tile_rows = pixels // LANES
    for k in range(tile_rows // 2):
        at = slice(2 * k * LANES, 2 * (k + 1) * LANES)
        hi, lo = hi_ref[:, at], lo_ref[:, at]
        part = product(xh_ref[...], hi, (1, 0)) + (
            product(xh_ref[...], lo, (1, 0)) + product(xl_ref[...], hi, (1, 0)) + product(xl_ref[...], lo, (1, 0)))
        for i in range(2):
            out32[pl.ds(2 * k + i, exposures, stride=tile_rows), :] = part[:, i * LANES:(i + 1) * LANES]
    b_ref[...] = out32[...].astype(jnp.bfloat16)


def solve(gram, hi, lo, pixel_total):
    exposures, pixels = hi.shape
    vm = pl.BlockSpec(memory_space=pltpu.VMEM)
    return pl.pallas_call(
        functools.partial(solve_kernel, pixel_total),
        out_shape=(
            jax.ShapeDtypeStruct((exposures, exposures), jnp.float32),
            jax.ShapeDtypeStruct((exposures * pixels // LANES, LANES), jnp.bfloat16),
        ),
        in_specs=[vm, vm, vm],
        out_specs=(vm, vm),
        scratch_shapes=[
            pltpu.VMEM((LANES, LANES), jnp.float32),
            pltpu.VMEM((exposures, exposures), jnp.bfloat16),
            pltpu.VMEM((exposures, exposures), jnp.bfloat16),
            pltpu.VMEM((exposures * pixels // LANES, LANES), jnp.float32),
        ],
    )(gram, hi, lo)


def per_device(frames, source_mask, good_pixels):
    exposures, tile_rows, tile_cols = frames.shape
    tiles = lax.axis_size("tile")
    pixel_total = float(tile_rows * tile_cols * lax.axis_size("ccd") * tiles)
    hi, lo, summed = exchange(frames, source_mask, good_pixels, column_matrix(tile_cols))
    factor, basis = solve(summed.reshape(3, LANES, LANES), hi, lo, pixel_total)
    return (factor, basis.reshape(exposures, tile_rows, tile_cols))


def solution(mesh):
    in_specs = (
        P(None, ("ccd", "tile"), None),
        P(None, ("ccd", "tile"), None),
        P(("ccd", "tile"), None),
    )
    out_specs = (P(), P(None, ("ccd", "tile"), None))
    return jax.shard_map(
        per_device, mesh=mesh, in_specs=in_specs, out_specs=out_specs, check_vma=False
    )
```
